32 devices in a mesh: heads: 2 (over x), blk: 16 (over z, y, core).
Axes of the slice: x: 2, y: 2, z: 4, core: 2. Of those that a mesh axis runs over, the one named last changes fastest.
Arguments:
- queries: bfloat16 [1024, 64, 128], P('blk', 'heads'), may hold values from -8 to 8
- prefix_keys: bfloat16 [8, 32768, 128], P('heads', 'blk'), may hold values from -8 to 8
- cached_prefix_values: bfloat16 [8, 32768, 128], P('heads', 'blk'), may hold values from -6 to 6
- shard_len: int32 [16], replicated, may hold values from 512 to 2048
- reach: int32 [16], replicated, may hold values from 4096 to 8192
- w_out: bfloat16 [8192, 16384], P('heads', 'blk'), may hold values from -0.0625 to 0.0625
Outputs:
- projected: bfloat16 [1024, 16384], P('heads', 'blk')
The draws below stay inside these ranges and needn't reach their ends.
All inputs are finite; a program needn't handle non-finite values.
Results may differ from the reference program's by a relative error of at most 0.0056.
Values may be sent and summed in bfloat16 or wider, within the bound.
A program may use at most 128 MiB of HBM per device.

```python
import jax
import jax.numpy as jnp
from jax import lax

D = 16384
QUERY_HEADS = 64
KEY_VALUE_HEADS = 8
HEAD_DIM = 128
QUERY_TOKENS = 64
KEYS_DEV = 2048
SPAN = 4
SHARDS = 16
TOKENS = 1024
PREFIX_SLOTS = 32768


def draw_queries(key, part):
    random_seed_key = jax.random.fold_in(key, 1)
    random_sample = jnp.clip(jax.random.normal(random_seed_key, (TOKENS, QUERY_HEADS, HEAD_DIM), jnp.float32), -6.0, 6.0)
    return random_sample.astype(jnp.bfloat16)


def draw_prefix_keys(key, part):
    random_seed_key = jax.random.fold_in(key, 2)
    random_sample = jnp.clip(jax.random.normal(random_seed_key, (KEY_VALUE_HEADS, PREFIX_SLOTS, HEAD_DIM), jnp.float32), -6.0, 6.0)
    return random_sample.astype(jnp.bfloat16)


def with_ends(values, stream_key, smallest, high):
    longest = values.shape.index(max(values.shape))
    spots = []
    for shift in (0, 1):
        where = [jax.random.randint(jax.random.fold_in(stream_key, axis), (), 0, length) for axis, length in enumerate(values.shape)]
        where[longest] = (where[longest] + shift) % values.shape[longest]
        spots.append(tuple(where))
    return values.at[spots[0]].set(smallest).at[spots[1]].set(high)


def steps_of(key, shape, cuts, low, top_value):
    gain, own = 1.0, jax.random.fold_in(key, 6)
    for axis_at, parts in cuts:
        draws = jnp.exp(jax.random.uniform(jax.random.fold_in(own, axis_at), (parts,), jnp.float32, low / len(cuts), top_value / len(cuts)))
        gain = gain * jnp.repeat(draws, shape[axis_at] // parts).reshape([-1 if axis == axis_at else 1 for axis in range(len(shape))])
    return gain


def scatter_about(key, dims, width, most, shards=(), kind=jnp.bfloat16):
    loudness = steps_of(key, dims, shards, -0.22, 0.18) if shards else 1.0
    values = jax.random.normal(key, dims, jnp.float32) * width * loudness
    return jnp.minimum(jnp.maximum(values, -most), most).astype(kind)


def setup_inputs(seed: int = 0) -> dict:
    splits = jax.random.split(jax.random.key(seed), 7)
    queries = draw_queries(jax.random.fold_in(splits[6], 71), 0)
    prefix_keys = draw_prefix_keys(jax.random.fold_in(splits[6], 71), 0)
    cached_prefix_values = scatter_about(splits[2], (KEY_VALUE_HEADS, PREFIX_SLOTS, HEAD_DIM), 1.0, 6.0, ((0, 2), (1, 16)))
    shard_len = with_ends(jax.random.randint(splits[3], (SHARDS,), KEYS_DEV // 4, KEYS_DEV + 1), jax.random.fold_in(splits[3], 1), KEYS_DEV // 4, KEYS_DEV).astype(jnp.int32)
    reach = with_ends(jax.random.randint(splits[4], (SHARDS,), SPAN * KEYS_DEV // 2, SPAN * KEYS_DEV + 1), jax.random.fold_in(splits[4], 1), SPAN * KEYS_DEV // 2, SPAN * KEYS_DEV).astype(jnp.int32)
    w_out = scatter_about(splits[5], (QUERY_HEADS * HEAD_DIM, D), (QUERY_HEADS * HEAD_DIM) ** -0.5, 0.0625, ((0, 2), (1, 16)))
    return {"queries": queries, "prefix_keys": prefix_keys, "cached_prefix_values": cached_prefix_values, "shard_len": shard_len, "reach": reach, "w_out": w_out}


masked_score = -1e30


def part_stats(query_tile_rows, key_block, value_block, visible):
    scores = jnp.einsum("thgd,hnd->thgn", query_tile_rows.astype(jnp.float32), key_block.astype(jnp.float32)) * (HEAD_DIM ** -0.5)
    visible_grid = visible[:, None, None, :]
    maxima = jnp.max(jnp.where(visible_grid, scores, masked_score), axis=-1)
    weights = jnp.where(visible_grid, jnp.exp(scores - maxima[..., None]), 0.0)
    totals = jnp.sum(weights, axis=-1)
    weighted = jnp.einsum("thgn,hnd->thgd", weights.astype(jnp.bfloat16).astype(jnp.float32), value_block.astype(jnp.float32))
    return maxima, totals, weighted


def combine_parts(first, second):
    joined = jnp.maximum(first[0], second[0])
    first_factor = jnp.exp(first[0] - joined)
    second_factor = jnp.exp(second[0] - joined)
    totals = first[1] * first_factor + second[1] * second_factor
    weighted = first[2] * first_factor[..., None] + second[2] * second_factor[..., None]
    return joined, totals, weighted


def reference(queries, prefix_keys, cached_prefix_values, shard_len, reach, w_out):
    heads_per_group = QUERY_HEADS // KEY_VALUE_HEADS
    row_ids = jnp.arange(QUERY_TOKENS, dtype=jnp.int32)[:, None]
    slot_ids = jnp.arange(KEYS_DEV, dtype=jnp.int32)[None, :]

    def block_attention(block_id):
        starting_row = (block_id * QUERY_TOKENS).astype(jnp.int32)
        query_tile_rows = lax.dynamic_slice_in_dim(queries, starting_row, QUERY_TOKENS, 0).reshape(QUERY_TOKENS, KEY_VALUE_HEADS, heads_per_group, HEAD_DIM)
        running = None
        for offset in range(SPAN):
            shard_id = ((block_id + offset) % SHARDS).astype(jnp.int32)
            first_slot = (shard_id * KEYS_DEV).astype(jnp.int32)
            key_block = lax.dynamic_slice_in_dim(prefix_keys, first_slot, KEYS_DEV, 1)
            value_block = lax.dynamic_slice_in_dim(cached_prefix_values, first_slot, KEYS_DEV, 1)
            visible = (slot_ids < shard_len[shard_id]) & (offset * KEYS_DEV + slot_ids < reach[block_id] + row_ids)
            partial_value = part_stats(query_tile_rows, key_block, value_block, visible)
            running = partial_value if offset == 0 else combine_parts(running, partial_value)
        attended = (running[2] / running[1][..., None]).astype(jnp.bfloat16)
        return attended.reshape(QUERY_TOKENS, QUERY_HEADS * HEAD_DIM)

    attended = lax.map(block_attention, jnp.arange(SHARDS, dtype=jnp.int32)).reshape(TOKENS, QUERY_HEADS * HEAD_DIM)
    return jnp.dot(attended, w_out, preferred_element_type=jnp.float32).astype(jnp.bfloat16)
```

```python
import functools
import math

import jax
import jax.numpy as jnp
from jax import lax
from jax.experimental import pallas as pl
from jax.experimental.pallas import tpu as pltpu
from jax.sharding import PartitionSpec as P

masked_score = -1e30

UNITS = 8
UNIT_SLOT = (0, 0, 2, 2, 1, 3, 3, 4)
UNIT_SHARD = (0, 1, 0, 1, 1, 0, 1, 0)
UNIT_FIRST = (1, 0, 1, 0, 1, 1, 0, 1)
UNIT_LAST = (0, 1, 0, 1, 1, 0, 1, 1)
SLOT_BLOCK = (0, 1, -2, -1, -3)
LEAD = 7


def pick(index, values):
    out = jnp.int32(values[-1])
    for n in range(len(values) - 2, -1, -1):
        out = jnp.where(index == n, jnp.int32(values[n]), out)
    return out


def layer_kernel(row_sets, rows, q_ref, k_ref, v_ref, live_ref, reach_ref, w_ref, o_ref,
                 q_all, k_all, v_all, run_max, run_sum, run_acc, own_part, own_stat,
                 part_out, stat_out, part_in, stat_in, buf, w_buf, acc, outgoing, incoming,
                 local_sem, w_sem, kv_send, kv_recv, q_send, q_recv, part_send, part_recv, stat_send, stat_recv,
                 col_send, col_recv, forward_send, pair_send, pair_recv, core_send, core_recv,
                 share_send, share_recv):
    splits = lax.axis_size("heads")
    count = lax.axis_size("blk")
    h = lax.axis_index("heads")
    me = lax.axis_index("blk")
    chips = count // 2
    chip, c = me // 2, me % 2
    r, p = chip // 2, chip % 2
    half = row_sets // 2
    _, kvh, lanes, head_size = q_ref.shape
    group = lanes // rows
    keys = k_ref.shape[1]
    kv_split = k_ref.shape[0] // kvh
    wide = group * head_size
    band = 4 * rows
    per_share = row_sets // splits
    columns = w_ref.shape[1]
    strip = min(256, columns)
    first = ((h + 1) % splits) * per_share
    chunks = 2 * kvh
    size = row_sets // 4 if row_sets >= 4 else 1
    groups = row_sets // size
    gateway = half - 1 + r // half
    other_gateway = half - r // half
    my_half = (r // half) * half

    def device(row_set, pair, core):
        return (row_set * 2 + pair) * 2 + core

    def remote(src, dst, sent, landed, head, blk):
        return pltpu.make_async_remote_copy(
            src_ref=src, dst_ref=dst, send_sem=sent, recv_sem=landed,
            device_id=(head, blk), device_id_type=pl.DeviceIdType.MESH,
        )

    def kv_half(core, i):
        return core * (kv_split - 1) * kvh + i

    def local(i):
        return [
            pltpu.make_async_copy(k_ref.at[kv_half(c, i)], k_all.at[c, i], local_sem.at[3 * i]),
            pltpu.make_async_copy(v_ref.at[kv_half(c, i)], v_all.at[c, i], local_sem.at[3 * i + 1]),
            pltpu.make_async_copy(q_ref.at[c, i], q_all.at[c, i], local_sem.at[3 * i + 2]),
        ]

    def swapped(i, shard):
        return [
            remote(k_ref.at[kv_half(1 - c, i)], k_all.at[shard, i], kv_send.at[3 * i], kv_recv.at[3 * i], h, me + 1 - 2 * c),
            remote(v_ref.at[kv_half(1 - c, i)], v_all.at[shard, i], kv_send.at[3 * i + 1], kv_recv.at[3 * i + 1], h, me + 1 - 2 * c),
            remote(q_ref.at[1 - c, i], q_all.at[shard, i], kv_send.at[3 * i + 2], kv_recv.at[3 * i + 2], h, me + 1 - 2 * c),
        ]

    def visit(i, core, slot, ahead):
        at = (i * 2 + core) * 2 + ahead - 1
        return remote(q_ref.at[core, i], q_all.at[slot, i], q_send.at[at], q_recv.at[(slot - 2) * kvh + i],
                      h, 2 * ((chip + ahead) % chips) + core)

    def part_home(v, i):
        back = 1 + v // 2
        return remote(part_out.at[v, i], part_in.at[v, i], part_send.at[v * kvh + i], part_recv.at[v * kvh + i],
                      h, 2 * ((chip - back + chips) % chips) + c)

    def stat_home(v, i):
        back = 1 + v // 2
        return remote(stat_out.at[v, i], stat_in.at[v, i], stat_send.at[v * kvh + i], stat_recv.at[v * kvh + i],
                      h, 2 * ((chip - back + chips) % chips) + c)

    def view(n, row_set, pair):
        at = device(row_set, pair, n % 2) * rows
        return buf.at[c * kvh + n // 2, pl.ds(pl.multiple_of(at, rows), rows), :]

    def to_column(n, row_set, target, sent):
        spot = view(n, row_set, p)
        return remote(spot, spot, sent, col_recv.at[n * row_sets + row_set], h, device(target, p, c))

    def to_pair(n, row_set, pair):
        spot = view(n, row_set, pair)
        at = n * row_sets + row_set
        return remote(spot, spot, pair_send.at[at], pair_recv.at[at], h, device(r, 1 - p, c))

    def to_core(i, row_set, core):
        at = pl.multiple_of(row_set * band, band)
        spot = buf.at[core * kvh + i, pl.ds(at, band), :]
        n = i * row_sets + row_set
        return remote(spot, spot, core_send.at[n], core_recv.at[n], h, device(r, p, 1 - c))

    def to_share(k):
        row_set = (first + k) % row_sets
        owner = row_set // per_share
        slot = ((h - owner + splits) % splits - 1) * per_share + row_set % per_share
        return remote(outgoing.at[k], incoming.at[slot], share_send.at[k], share_recv.at[slot], owner, me)

    def from_share(slot):
        return remote(outgoing.at[0], incoming.at[slot], share_send.at[0], share_recv.at[slot], (h + 1) % splits, me)

    def own_targets(n):
        copies = [(to_column(n, r, my_half + (r - my_half + d) % half, col_send.at[n * half + d - 1]))
                  for d in range(1, half)]
        return copies + [to_column(n, r, other_gateway, col_send.at[n * half + half - 1])]

    def forwards(n, row_set):
        base = (n * half + row_set % half) * half
        return [to_column(n, row_set, my_half + (r - my_half + d) % half, forward_send.at[base + d])
                for d in range(1, half)]

    for i in range(kvh):
        for copy in local(i):
            copy.start()
    greeted = [(h, device((r + d) % row_sets, p, c)) for d in range(1, row_sets)]
    greeted += [(h, device(r, 1 - p, c)), (h, me + 1 - 2 * c)]
    greeted += [((h + d) % splits, me) for d in range(1, splits)]
    for d in (1, 2, chips - 2, chips - 1):
        greeted += [(h, 2 * ((chip + d) % chips) + core) for core in range(2)]
    barrier = pltpu.get_barrier_semaphore()
    for peer in greeted:
        pl.semaphore_signal(barrier, inc=1, device_id=peer, device_id_type=pl.DeviceIdType.MESH)
    pl.semaphore_wait(barrier, len(greeted))
    for i in range(kvh):
        for copy in swapped(i, c):
            copy.start()
        for core in range(2):
            visit(i, core, 2 + c, 1).start()

            @pl.when(c == 1)
            def _():
                visit(i, core, 4, 2).start()

    w_copy = pltpu.make_async_copy(w_ref, w_buf, w_sem.at[0])
    w_copy.start()

    factor = head_size**-0.5 * math.log2(math.e)

    def attend(u, i):
        slot, shard = pick(u, UNIT_SLOT), pick(u, UNIT_SHARD)
        ahead = pick(slot, SLOT_BLOCK)
        owner = (2 * chip + ahead + count) % count
        edge = reach_ref[owner] - (shard - ahead) * keys
        live = live_ref[2 * chip + shard]
        token = lax.broadcasted_iota(jnp.int32, (1, lanes), 1) % rows
        limit = jnp.minimum(edge + token, live)
        seen = lax.broadcasted_iota(jnp.int32, (keys, lanes), 0) < limit
        s = lax.dot_general(
            k_all[shard, i], q_all[slot, i], (((1,), (1,)), ((), ())), preferred_element_type=jnp.float32
        )
        s = jnp.where(seen, s * factor, masked_score)
        m = jnp.max(s, axis=0, keepdims=True)
        weight = jnp.exp2(s - m)
        total = jnp.sum(weight, axis=0, keepdims=True)
        part = lax.dot_general(
            v_all[shard, i], weight.astype(jnp.bfloat16), (((0,), (0,)), ((), ())),
            preferred_element_type=jnp.float32,
        )
        begins, ends = pick(u, UNIT_FIRST), pick(u, UNIT_LAST)

        @pl.when(begins == 1)
        def _():
            run_max[...] = jnp.broadcast_to(m, run_max.shape)
            run_sum[...] = jnp.broadcast_to(total, run_sum.shape)
            run_acc[...] = part

        @pl.when(begins == 0)
        def _():
            before = run_max[:1, :]
            joined = jnp.maximum(before, m)
            old, new = jnp.exp2(before - joined), jnp.exp2(m - joined)
            run_max[...] = jnp.broadcast_to(joined, run_max.shape)
            run_sum[...] = jnp.broadcast_to(run_sum[:1, :] * old + total * new, run_sum.shape)
            run_acc[...] = run_acc[...] * old + part * new

        @pl.when((ends == 1) & (slot < 2))
        def _():
            own_part[slot, i] = run_acc[...] * (1.0 / run_sum[:1, :])
            own_stat[slot, i] = run_max[...] + jnp.log2(run_sum[...])

        @pl.when((ends == 1) & (slot >= 2))
        def _():
            part_out[slot - 2, i] = (run_acc[...] * (1.0 / run_sum[:1, :])).astype(part_out.dtype)
            stat_out[slot - 2, i] = run_max[...] + jnp.log2(run_sum[...])

    def merge(i, e):
        arrived = [e] if e == 0 else [1, 2]
        for v in arrived:
            part_home(v, i).wait_recv()
            stat_home(v, i).wait_recv()
        stats = [own_stat[e, i, :1, :]] + [stat_in[v, i, :1, :] for v in arrived]
        joined = functools.reduce(jnp.maximum, stats)
        weights = [jnp.exp2(s - joined) for s in stats]
        inverse = 1.0 / functools.reduce(jnp.add, weights)
        total = own_part[e, i] * (weights[0] * inverse)
        for v, weight in zip(arrived, weights[1:]):
            total = total + part_in[v, i].astype(jnp.float32) * (weight * inverse)
        total = total.T.astype(jnp.bfloat16)
        spot = pl.ds(pl.multiple_of((2 * chip + e) * rows, rows), rows)
        for g in range(group):
            buf[c * kvh + i, spot, g * head_size : (g + 1) * head_size] = total[g * rows : (g + 1) * rows]
        n = 2 * i + e
        for copy in own_targets(n):
            copy.start()
        to_pair(n, r, p).start()

    def direct(row_set):
        return (row_set // half == r // half) | (r == gateway)

    def relay_one(n, row_set):
        to_column(n, row_set, r, col_send.at[0]).wait_recv()
        to_pair(n, row_set, p).start()

        @pl.when((row_set // half != r // half) & (r == gateway))
        def _():
            for copy in forwards(n, row_set):
                copy.start()

    def relay(t):
        for lag in range(2):
            at = t - lag
            n, g = at // groups, at % groups

            def some(j, carry):
                row_set = (first + g * size + j) % row_sets
                wanted = direct(row_set) if lag == 0 else jnp.logical_not(direct(row_set))

                @pl.when(wanted & (row_set != r))
                def _():
                    relay_one(n, row_set)

                return carry

            @pl.when((at >= 0) & (at < chunks * groups))
            def _():
                lax.fori_loop(0, size, some, 0)

    def unit(s, carry):
        u, i = s % UNITS, s // UNITS

        @pl.when(u == 0)
        def _():
            for copy in local(i):
                copy.wait()
            for copy in swapped(i, 1 - c):
                copy.wait_recv()

        for at, slot in ((2, 2), (5, 3), (7, 4)):
            @pl.when(u == at)
            def _():
                visit(i, 0, slot, 1).wait_recv()

        attend(u, i)
        for at, v in ((3, 0), (6, 1), (7, 2)):
            @pl.when(u == at)
            def _():
                part_home(v, i).start()
                stat_home(v, i).start()

        @pl.when(u == 5)
        def _():
            merge(i, 0)

        @pl.when((u == 1) & (s >= UNITS))
        def _():
            merge(i - 1, 1)

        relay(s - LEAD)
        return carry

    steps = UNITS * kvh
    lax.fori_loop(0, steps, unit, 0)
    merge(kvh - 1, 1)
    w_copy.wait()

    final = steps + max(5, 4 * (kvh - 1) + 1)

    def place(s):
        early = s < final
        at = jnp.where(early, s - steps, s - final)
        i = jnp.where(early, at // groups, kvh - 1)
        ready = (at >= 0) & jnp.where(early, at < (kvh - 1) * groups, at < groups)
        return ready, i, at % groups

    def spread(i, g):
        def some(j, carry):
            row_set = (first + g * size + j) % row_sets
            for e in range(2):
                to_pair(2 * i + e, row_set, 1 - p).wait_recv()
            to_core(i, row_set, c).start()
            return carry

        lax.fori_loop(0, size, some, 0)

    def project(i, g):
        def some(j, carry):
            k = g * size + j
            row_set = (first + k) % row_sets
            to_core(i, row_set, 1 - c).wait_recv()
            at = pl.multiple_of(row_set * band, band)

            def multiply(n, carry):
                cols = pl.ds(pl.multiple_of(n * strip, strip), strip)
                value = sum(
                    jnp.dot(
                        buf[core * kvh + i, pl.ds(at, band), :],
                        w_buf[pl.ds(pl.multiple_of((core * kvh + i) * wide, wide), wide), cols],
                        preferred_element_type=jnp.float32,
                    )
                    for core in range(2)
                )

                @pl.when(i == 0)
                def _():
                    acc[k, :, cols] = value

                @pl.when(i > 0)
                def _():
                    acc[k, :, cols] += value

                return carry

            lax.fori_loop(0, columns // strip, multiply, 0)

            @pl.when((i == kvh - 1) & (k < row_sets - per_share))
            def _():
                outgoing[k] = acc[k].astype(outgoing.dtype)
                to_share(k).start()

            @pl.when((i == kvh - 1) & (k >= row_sets - per_share))
            def _():
                slot = row_set % per_share
                value = acc[k]
                for d in range(splits - 1):
                    from_share(d * per_share + slot).wait_recv()
                    value = value + incoming[d * per_share + slot].astype(jnp.float32)
                o_ref[pl.ds(pl.multiple_of(slot * band, band), band), :] = value.astype(o_ref.dtype)

            return carry

        lax.fori_loop(0, size, some, 0)

    def drain_step(s, carry):
        relay(s - LEAD)
        ready, i, g = place(s)

        @pl.when(ready)
        def _():
            spread(i, g)

        ready, i, g = place(s - 1)

        @pl.when(ready)
        def _():
            project(i, g)

        return carry

    lax.fori_loop(steps, final + groups + 1, drain_step, 0)

    for i in range(kvh):
        for copy in swapped(i, c):
            copy.wait_send()
        for core in range(2):
            visit(i, core, 2 + c, 1).wait_send()

            @pl.when(c == 1)
            def _():
                visit(i, core, 4, 2).wait_send()

        for v in range(3):
            part_home(v, i).wait_send()
            stat_home(v, i).wait_send()

    def drain_sent(n, carry):
        for copy in own_targets(n):
            copy.wait_send()

        def some(row_set, carry):
            to_pair(n, row_set, p).wait_send()

            @pl.when((row_set // half != r // half) & (r == gateway))
            def _():
                for copy in forwards(n, row_set):
                    copy.wait_send()

            return carry

        return lax.fori_loop(0, row_sets, some, carry)

    lax.fori_loop(0, chunks, drain_sent, 0)

    def drain_core(n, carry):
        to_core(n // row_sets, n % row_sets, c).wait_send()
        return carry

    lax.fori_loop(0, kvh * row_sets, drain_core, 0)

    def drain_share(k, carry):
        to_share(k).wait_send()
        return carry

    lax.fori_loop(0, row_sets - per_share, drain_share, 0)


def on_device(queries, prefix_keys, cached_prefix_values, shard_len, reach, w_out):
    count, splits = lax.axis_size("blk"), lax.axis_size("heads")
    rows, heads_local, head_size = queries.shape
    kv_local, keys_len = prefix_keys.shape[:2]
    kvh = kv_local // 2 if kv_local % 2 == 0 else kv_local
    group = heads_local // 2 // kvh
    lanes = group * rows
    columns = w_out.shape[1]
    row_sets = count // 4
    half = row_sets // 2
    per_share = row_sets // splits
    band = 4 * rows
    chunks = 2 * kvh
    q = queries.reshape(rows, 2, kvh, group, head_size).transpose(1, 2, 3, 0, 4).reshape(2, kvh, lanes, head_size)
    dma = pltpu.SemaphoreType.DMA
    bf16, f32 = jnp.bfloat16, jnp.float32
    anywhere = pl.BlockSpec(memory_space=pl.ANY)
    scalars = pl.BlockSpec(memory_space=pltpu.SMEM)
    visits = dma((3 * kvh,))
    sets = dma((chunks * row_sets,))
    return pl.pallas_call(
        functools.partial(layer_kernel, row_sets, rows),
        out_shape=jax.ShapeDtypeStruct((per_share * band, columns), bf16),
        in_specs=[anywhere, anywhere, anywhere, scalars, scalars, anywhere],
        out_specs=pl.BlockSpec(memory_space=pltpu.VMEM),
        scratch_shapes=[
            pltpu.VMEM((5, kvh, lanes, head_size), bf16),
            pltpu.VMEM((2, kvh, keys_len, head_size), bf16),
            pltpu.VMEM((2, kvh, keys_len, head_size), bf16),
            pltpu.VMEM((8, lanes), f32),
            pltpu.VMEM((8, lanes), f32),
            pltpu.VMEM((head_size, lanes), f32),
            pltpu.VMEM((2, kvh, head_size, lanes), f32),
            pltpu.VMEM((2, kvh, 8, lanes), f32),
            pltpu.VMEM((3, kvh, head_size, lanes), bf16),
            pltpu.VMEM((3, kvh, 8, lanes), f32),
            pltpu.VMEM((3, kvh, head_size, lanes), bf16),
            pltpu.VMEM((3, kvh, 8, lanes), f32),
            pltpu.VMEM((2 * kvh, count * rows, group * head_size), bf16),
            pltpu.VMEM(w_out.shape, bf16),
            pltpu.VMEM((row_sets, band, columns), f32),
            pltpu.VMEM((row_sets - per_share, band, columns), bf16),
            pltpu.VMEM((row_sets - per_share, band, columns), bf16),
            dma((3 * kvh,)),
            dma((1,)),
            dma((3 * kvh,)),
            dma((3 * kvh,)),
            dma((4 * kvh,)),
            visits, visits, visits, visits, visits,
            dma((chunks * half,)),
            sets,
            dma((chunks * half * half,)),
            sets, sets,
            dma((kvh * row_sets,)),
            dma((kvh * row_sets,)),
            dma((row_sets - per_share,)),
            dma((row_sets - per_share,)),
        ],
        compiler_params=pltpu.CompilerParams(
            collective_id=0, has_side_effects=True, vmem_limit_bytes=60 << 20
        ),
    )(q, prefix_keys, cached_prefix_values, shard_len, reach, w_out)


def solution(mesh):
    return jax.shard_map(
        on_device,
        mesh=mesh,
        in_specs=(
            P("blk", "heads", None),
            P("heads", "blk", None),
            P("heads", "blk", None),
            P(),
            P(),
            P("heads", "blk"),
        ),
        out_specs=P("heads", "blk"),
        check_vma=False,
    )
```

```python
import functools
import math

import jax
import jax.numpy as jnp
from jax import lax
from jax.experimental import pallas as pl
from jax.experimental.pallas import tpu as pltpu
from jax.sharding import PartitionSpec as P

masked_score = -1e30

LOCAL = (((0, 0, 1, 0),), ((1, 1, 1, 1),))
OWN = (((0, 1, 0, 1), (1, 1, 1, 1)), ((0, 0, 1, 0), (0, 1, 0, 1)))
VISIT = ((2, 0, 1, 0), (2, 1, 0, 1), (3, 0, 1, 0), (3, 1, 0, 1), (4, 0, 1, 1))
SLOT_BLOCK = (0, 1, -2, -1, -3)


def pick(index, values):
    out = jnp.int32(values[-1])
    for n in range(len(values) - 2, -1, -1):
        out = jnp.where(index == n, jnp.int32(values[n]), out)
    return out


def layer_kernel(row_sets, rows, q_ref, k_ref, v_ref, live_ref, reach_ref, w_ref, o_ref,
                 q_all, k_all, v_all, run_max, run_sum, run_acc, own_part, own_stat,
                 part_out, stat_out, part_in, stat_in, buf, w_buf, acc, outgoing, incoming,
                 local_sem, w_sem, kv_send, kv_recv, q_send, q_recv, part_send, part_recv, stat_send, stat_recv,
                 col_send, col_recv, forward_send, pair_send, pair_recv, core_send, core_recv,
                 share_send, share_recv):
    splits = lax.axis_size("heads")
    count = lax.axis_size("blk")
    h = lax.axis_index("heads")
    me = lax.axis_index("blk")
    chips = count // 2
    chip, c = me // 2, me % 2
    r, p = chip // 2, chip % 2
    half = row_sets // 2
    _, kvh, lanes, head_size = q_ref.shape
    group = lanes // rows
    keys = k_ref.shape[1]
    kv_split = k_ref.shape[0] // kvh
    wide = group * head_size
    band = 4 * rows
    per_share = row_sets // splits
    share_rows = 2 * per_share * rows
    columns = w_ref.shape[1]
    strip = min(1024, columns)
    first = ((h + 1) % splits) * per_share
    chunks = 2 * kvh
    outgoing_sets = row_sets - per_share
    outgoing_half = (outgoing_sets + 1) // 2
    gateway = half - 1 + r // half
    other_gateway = half - r // half
    my_half = (r // half) * half

    def device(row_set, pair, core):
        return (row_set * 2 + pair) * 2 + core

    def remote(src, dst, sent, landed, head, blk):
        return pltpu.make_async_remote_copy(
            src_ref=src, dst_ref=dst, send_sem=sent, recv_sem=landed,
            device_id=(head, blk), device_id_type=pl.DeviceIdType.MESH,
        )

    def kv_half(core, i):
        return core * (kv_split - 1) * kvh + i

    def local(i):
        return [
            pltpu.make_async_copy(k_ref.at[kv_half(c, i)], k_all.at[c, i], local_sem.at[3 * i]),
            pltpu.make_async_copy(v_ref.at[kv_half(c, i)], v_all.at[c, i], local_sem.at[3 * i + 1]),
            pltpu.make_async_copy(q_ref.at[c, i], q_all.at[c, i], local_sem.at[3 * i + 2]),
        ]

    def swapped(i, shard):
        return [
            remote(k_ref.at[kv_half(1 - c, i)], k_all.at[shard, i], kv_send.at[3 * i], kv_recv.at[3 * i], h, me + 1 - 2 * c),
            remote(v_ref.at[kv_half(1 - c, i)], v_all.at[shard, i], kv_send.at[3 * i + 1], kv_recv.at[3 * i + 1], h, me + 1 - 2 * c),
            remote(q_ref.at[1 - c, i], q_all.at[shard, i], kv_send.at[3 * i + 2], kv_recv.at[3 * i + 2], h, me + 1 - 2 * c),
        ]

    def visit(i, core, slot, ahead):
        at = (i * 2 + core) * 2 + ahead - 1
        return remote(q_ref.at[core, i], q_all.at[slot, i], q_send.at[at], q_recv.at[(slot - 2) * kvh + i],
                      h, 2 * ((chip + ahead) % chips) + core)

    def part_home(v, i):
        back = 1 + v // 2
        return remote(part_out.at[v, i], part_in.at[v, i], part_send.at[v * kvh + i], part_recv.at[v * kvh + i],
                      h, 2 * ((chip - back + chips) % chips) + c)

    def stat_home(v, i):
        back = 1 + v // 2
        return remote(stat_out.at[v, i], stat_in.at[v, i], stat_send.at[v * kvh + i], stat_recv.at[v * kvh + i],
                      h, 2 * ((chip - back + chips) % chips) + c)

    def view(n, row_set, pair):
        at = (((n % 2) * row_sets + row_set) * 2 + pair) * rows
        return buf.at[c * kvh + n // 2, pl.ds(pl.multiple_of(at, rows), rows), :]

    def to_column(n, row_set, target, sent):
        spot = view(n, row_set, p)
        return remote(spot, spot, sent, col_recv.at[n * row_sets + row_set], h, device(target, p, c))

    def to_pair(n, row_set, pair):
        spot = view(n, row_set, pair)
        at = n * row_sets + row_set
        return remote(spot, spot, pair_send.at[at], pair_recv.at[at], h, device(r, 1 - p, c))

    def to_core(n, row_set, core):
        at = pl.multiple_of(((n % 2) * row_sets + row_set) * 2 * rows, 2 * rows)
        spot = buf.at[core * kvh + n // 2, pl.ds(at, 2 * rows), :]
        at = n * row_sets + row_set
        return remote(spot, spot, core_send.at[at], core_recv.at[at], h, device(r, p, 1 - c))

    def to_share(e, j):
        owner = (h + 1 + j) % splits
        slot = e * (splits - 1) + splits - 2 - j
        return remote(outgoing.at[e, j], incoming.at[slot], share_send.at[e * (splits - 1) + j], share_recv.at[slot],
                      owner, me)

    def from_share(slot):
        return remote(outgoing.at[0, 0], incoming.at[slot], share_send.at[0], share_recv.at[slot],
                      (h + 1) % splits, me)

    def unicast(n):
        return n < 0

    def own_columns(n, act):
        for d in range(1, row_sets):
            target = (r + d) % row_sets

            @pl.when((target // half == r // half) | (target == other_gateway) | unicast(n))
            def _():
                act(to_column(n, r, target, col_send.at[n * row_sets + d]))

    def forwards(n, row_set):
        base = (n * half + row_set % half) * half
        return [to_column(n, row_set, my_half + (r - my_half + d) % half, forward_send.at[base + d])
                for d in range(1, half)]

    for i in range(kvh):
        for copy in local(i):
            copy.start()
    greeted = [(h, device((r + d) % row_sets, p, c)) for d in range(1, row_sets)]
    greeted += [(h, device(r, 1 - p, c)), (h, me + 1 - 2 * c)]
    greeted += [((h + d) % splits, me) for d in range(1, splits)]
    for d in (1, 2, chips - 2, chips - 1):
        greeted += [(h, 2 * ((chip + d) % chips) + core) for core in range(2)]
    barrier = pltpu.get_barrier_semaphore()
    for peer in greeted:
        pl.semaphore_signal(barrier, inc=1, device_id=peer, device_id_type=pl.DeviceIdType.MESH)
    def start_visits(i):
        for core in range(2):
            visit(i, core, 2 + c, 1).start()

            @pl.when(c == 1)
            def _():
                visit(i, core, 4, 2).start()

    w_copy = pltpu.make_async_copy(w_ref, w_buf, w_sem.at[0])

    factor = head_size**-0.5 * math.log2(math.e)

    last = kvh - 1

    def attend(i, what):
        slot, shard, begins, ends = what
        held = jnp.where(slot < 2, i, kvh)
        ahead = pick(slot, SLOT_BLOCK)
        owner = (2 * chip + ahead + count) % count
        edge = reach_ref[owner] - (shard - ahead) * keys
        live = live_ref[2 * chip + shard]
        token = lax.broadcasted_iota(jnp.int32, (1, lanes), 1) % rows
        limit = jnp.minimum(edge + token, live)
        seen = lax.broadcasted_iota(jnp.int32, (keys, lanes), 0) < limit
        s = lax.dot_general(
            k_all[shard, i], q_all[slot, i], (((1,), (1,)), ((), ())), preferred_element_type=jnp.float32
        )
        s = jnp.where(seen, s * factor, masked_score)
        m = jnp.max(s, axis=0, keepdims=True)
        weight = jnp.exp2(s - m)
        total = jnp.sum(weight, axis=0, keepdims=True)
        part = lax.dot_general(
            v_all[shard, i], weight.astype(jnp.bfloat16), (((0,), (0,)), ((), ())),
            preferred_element_type=jnp.float32,
        )

        @pl.when(begins == 1)
        def _():
            run_max[held] = jnp.broadcast_to(m, run_max.shape[1:])
            run_sum[held] = jnp.broadcast_to(total, run_sum.shape[1:])
            run_acc[held] = part

        @pl.when(begins == 0)
        def _():
            before = run_max[held, :1, :]
            joined = jnp.maximum(before, m)
            old, new = jnp.exp2(before - joined), jnp.exp2(m - joined)
            run_max[held] = jnp.broadcast_to(joined, run_max.shape[1:])
            run_sum[held] = jnp.broadcast_to(run_sum[held, :1, :] * old + total * new, run_sum.shape[1:])
            run_acc[held] = run_acc[held] * old + part * new

        @pl.when((ends == 1) & (slot < 2))
        def _():
            own_part[slot, i] = run_acc[held] * (1.0 / run_sum[held, :1, :])
            own_stat[slot, i] = run_max[held] + jnp.log2(run_sum[held])

        @pl.when((ends == 1) & (slot >= 2))
        def _():
            part_out[slot - 2, i] = (run_acc[held] * (1.0 / run_sum[held, :1, :])).astype(part_out.dtype)
            stat_out[slot - 2, i] = run_max[held] + jnp.log2(run_sum[held])

    def merge(i, e):
        arrived = [e] if e == 0 else [1, 2]
        for v in arrived:
            part_home(v, i).wait_recv()
            stat_home(v, i).wait_recv()
        stats = [own_stat[e, i, :1, :]] + [stat_in[v, i, :1, :] for v in arrived]
        joined = functools.reduce(jnp.maximum, stats)
        weights = [jnp.exp2(s - joined) for s in stats]
        inverse = 1.0 / functools.reduce(jnp.add, weights)
        total = own_part[e, i] * (weights[0] * inverse)
        for v, weight in zip(arrived, weights[1:]):
            total = total + part_in[v, i].astype(jnp.float32) * (weight * inverse)
        total = total.T.astype(jnp.bfloat16)
        spot = pl.ds(pl.multiple_of(((e * row_sets + r) * 2 + p) * rows, rows), rows)
        for g in range(group):
            buf[c * kvh + i, spot, g * head_size : (g + 1) * head_size] = total[g * rows : (g + 1) * rows]
        n = 2 * i + e
        own_columns(n, lambda copy: copy.start())
        if not (i is last and e == 1):
            to_pair(n, r, p).start()

    def direct(n, row_set):
        return (row_set // half == r // half) | (r == gateway) | unicast(n)

    def relay_one(n, row_set):
        to_column(n, row_set, r, col_send.at[0]).wait_recv()
        to_pair(n, row_set, p).start()

        @pl.when((row_set // half != r // half) & (r == gateway) & jnp.logical_not(unicast(n)))
        def _():
            for copy in forwards(n, row_set):
                copy.start()

    def relay_some(n, start, stop, direct_now, own_too=False):
        def some(k, carry):
            row_set = (first + k) % row_sets

            @pl.when((direct(n, row_set) == direct_now) & (row_set != r))
            def _():
                relay_one(n, row_set)

            if direct_now and own_too:
                @pl.when(row_set == r)
                def _():
                    to_pair(n, r, p).start()

            return carry

        lax.fori_loop(start, stop, some, 0)

    def relay_all(n, start, stop, own_too=False):
        relay_some(n, start, stop, True, own_too)
        relay_some(n, start, stop, False)

    here, span = kvh, len(OWN[0]) + len(VISIT)
    steps = here + span * kvh

    def unit(s, carry):
        early = s < here
        i = jnp.where(early, s, (s - here) // span)
        j = jnp.where(early, 0, (s - here) % span)
        j = jnp.where(i < last, j, (j + len(OWN[0])) % span)
        own = jnp.logical_not(early) & (j < len(OWN[0]))
        visiting = jnp.logical_not(early) & (j >= len(OWN[0]))
        j = jnp.where(visiting, j - len(OWN[0]), j)

        @pl.when(early)
        def _():
            for copy in local(i):
                copy.wait()

        @pl.when(s == here)
        def _():
            pl.semaphore_wait(barrier, len(greeted))
            for copy in swapped(0, c):
                copy.start()
            start_visits(0)

        for n in range(1, kvh):
            @pl.when(s == here + 1 + span * (n - 1))
            def _():
                for copy in swapped(n, c):
                    copy.start()

            @pl.when(s == here + 3 + span * (n - 1))
            def _():
                start_visits(n)

        @pl.when(s == here + 4)
        def _():
            w_copy.start()

        @pl.when(jnp.logical_not(early) & ((s - here) % span == 0))
        def _():
            for copy in swapped(i, 1 - c):
                copy.wait_recv()

        for at, slot in ((0, 2), (2, 3), (4, 4)):
            @pl.when(visiting & (j == at))
            def _():
                visit(i, 0, slot, 1).wait_recv()

        def choose(field):
            local_one = pick(c, [LOCAL[core][0][field] for core in range(2)])
            own_one = pick(2 * c + j, [OWN[core][n][field] for core in range(2) for n in range(2)])
            visit_one = pick(j, [what[field] for what in VISIT])
            return jnp.where(early, local_one, jnp.where(own, own_one, visit_one))

        attend(i, [choose(field) for field in range(4)])
        for at, v in ((1, 0), (3, 1), (4, 2)):
            @pl.when(visiting & (j == at))
            def _():
                part_home(v, i).start()
                stat_home(v, i).start()

        @pl.when(visiting & (j == 0) & (i > 0))
        def _():
            merge(i - 1, 0)

        @pl.when(visiting & (j == 3) & (i > 0))
        def _():
            merge(i - 1, 1)

        @pl.when(visiting & (j == 4) & (i > 0))
        def _():
            relay_some(2 * i - 2, 0, outgoing_sets, True)

        @pl.when(own & (j == 0) & (i == last) & (i > 0))
        def _():
            relay_some(2 * i - 2, 0, outgoing_sets, False)
            relay_some(2 * i - 2, outgoing_sets, row_sets, True)

        @pl.when(own & (j == 1) & (i == last))
        def _():
            merge(i, 0)

            @pl.when(i > 0)
            def _():
                relay_some(2 * i - 2, outgoing_sets, row_sets, False)
                relay_some(2 * i - 1, 0, row_sets, True)

        return carry

    lax.fori_loop(0, steps, unit, 0)
    late = chunks - 2
    def over(start, stop, act):
        def some(k, carry):
            act(k)
            return carry

        lax.fori_loop(start, stop, some, 0)

    def spread(n, start, stop):
        def some(k):
            row_set = (first + k) % row_sets
            to_pair(n, row_set, 1 - p).wait_recv()
            to_core(n, row_set, c).start()

        over(start, stop, some)

    def project(n, j):
        i, e = n // 2, n % 2
        owner = (h + 1 + j) % splits
        over(0, per_share, lambda x: to_core(n, owner * per_share + x, 1 - c).wait_recv())
        at = pl.multiple_of((e * row_sets + owner * per_share) * 2 * rows, 2 * rows)

        def multiply(n, carry):
            cols = pl.ds(pl.multiple_of(n * strip, strip), strip)
            value = sum(
                jnp.dot(
                    buf[core * kvh + i, pl.ds(at, share_rows), :],
                    w_buf[pl.ds(pl.multiple_of((core * kvh + i) * wide, wide), wide), cols],
                    preferred_element_type=jnp.float32,
                )
                for core in range(2)
            )

            @pl.when(i == 0)
            def _():
                acc[e, j, :, cols] = value

            @pl.when(i > 0)
            def _():
                acc[e, j, :, cols] += value

            return carry

        lax.fori_loop(0, columns // strip, multiply, 0)

    def send_share(e):
        def some(j):
            outgoing[e, j] = acc[e, j].astype(outgoing.dtype)
            to_share(e, j).start()

        over(0, splits - 1, some)

    def take_share(e):
        value = acc[e, splits - 1]
        for d in range(splits - 1):
            slot = e * (splits - 1) + d
            from_share(slot).wait_recv()
            value = value + incoming[slot].astype(jnp.float32)
        value = value.astype(o_ref.dtype)
        for x in range(per_share):
            for pair in range(2):
                at = x * band + (2 * pair + e) * rows
                o_ref[at : at + rows, :] = value[(2 * x + pair) * rows : (2 * x + pair + 1) * rows]

    def project_out(n):
        over(0, splits - 1, lambda j: project(n, j))

    if kvh > 1:
        relay_some(late - 1, 0, row_sets, False)
    merge(last, 1)
    relay_all(late, 0, outgoing_sets)
    w_copy.wait()
    for n in range(0, late, 2):
        spread(n, 0, outgoing_sets)
        project_out(n)
    relay_some(chunks - 1, 0, outgoing_sets, True, True)
    spread(late, 0, outgoing_sets)
    relay_some(chunks - 1, 0, outgoing_sets, False)
    project_out(late)
    send_share(0)
    for n in range(1, late, 2):
        spread(n, 0, outgoing_sets)
        project_out(n)
    relay_all(late, outgoing_sets, row_sets)
    spread(chunks - 1, 0, outgoing_sets)
    project_out(chunks - 1)
    send_share(1)
    relay_all(chunks - 1, outgoing_sets, row_sets, True)
    over(0, late, lambda n: spread(n, outgoing_sets, row_sets))
    over(0, late, lambda n: project(n, splits - 1))
    spread(late, outgoing_sets, row_sets)
    project(late, splits - 1)
    spread(chunks - 1, outgoing_sets, row_sets)
    take_share(0)
    project(chunks - 1, splits - 1)
    take_share(1)

    for i in range(kvh):
        for copy in swapped(i, c):
            copy.wait_send()
        for core in range(2):
            visit(i, core, 2 + c, 1).wait_send()

            @pl.when(c == 1)
            def _():
                visit(i, core, 4, 2).wait_send()

        for v in range(3):
            part_home(v, i).wait_send()
            stat_home(v, i).wait_send()

    def drain_sent(n, carry):
        own_columns(n, lambda copy: copy.wait_send())

        def some(row_set, carry):
            to_pair(n, row_set, p).wait_send()

            @pl.when((row_set // half != r // half) & (r == gateway) & jnp.logical_not(unicast(n)))
            def _():
                for copy in forwards(n, row_set):
                    copy.wait_send()

            return carry

        return lax.fori_loop(0, row_sets, some, carry)

    lax.fori_loop(0, chunks, drain_sent, 0)

    def drain_core(n, carry):
        to_core(n // row_sets, n % row_sets, c).wait_send()
        return carry

    lax.fori_loop(0, chunks * row_sets, drain_core, 0)

    for e in range(2):
        for j in range(splits - 1):
            to_share(e, j).wait_send()


def on_device(queries, prefix_keys, cached_prefix_values, shard_len, reach, w_out):
    count, splits = lax.axis_size("blk"), lax.axis_size("heads")
    rows, heads_local, head_size = queries.shape
    kv_local, keys_len = prefix_keys.shape[:2]
    kvh = kv_local // 2 if kv_local % 2 == 0 else kv_local
    group = heads_local // 2 // kvh
    lanes = group * rows
    columns = w_out.shape[1]
    row_sets = count // 4
    half = row_sets // 2
    per_share = row_sets // splits
    band = 4 * rows
    share_rows = 2 * per_share * rows
    chunks = 2 * kvh
    q = queries.reshape(rows, 2, kvh, group, head_size).transpose(1, 2, 3, 0, 4).reshape(2, kvh, lanes, head_size)
    dma = pltpu.SemaphoreType.DMA
    bf16, f32 = jnp.bfloat16, jnp.float32
    anywhere = pl.BlockSpec(memory_space=pl.ANY)
    scalars = pl.BlockSpec(memory_space=pltpu.SMEM)
    visits = dma((3 * kvh,))
    sets = dma((chunks * row_sets,))
    return pl.pallas_call(
        functools.partial(layer_kernel, row_sets, rows),
        out_shape=jax.ShapeDtypeStruct((per_share * band, columns), bf16),
        in_specs=[anywhere, anywhere, anywhere, scalars, scalars, anywhere],
        out_specs=pl.BlockSpec(memory_space=pltpu.VMEM),
        scratch_shapes=[
            pltpu.VMEM((5, kvh, lanes, head_size), bf16),
            pltpu.VMEM((2, kvh, keys_len, head_size), bf16),
            pltpu.VMEM((2, kvh, keys_len, head_size), bf16),
            pltpu.VMEM((kvh + 1, 8, lanes), f32),
            pltpu.VMEM((kvh + 1, 8, lanes), f32),
            pltpu.VMEM((kvh + 1, head_size, lanes), f32),
            pltpu.VMEM((2, kvh, head_size, lanes), f32),
            pltpu.VMEM((2, kvh, 8, lanes), f32),
            pltpu.VMEM((3, kvh, head_size, lanes), bf16),
            pltpu.VMEM((3, kvh, 8, lanes), f32),
            pltpu.VMEM((3, kvh, head_size, lanes), bf16),
            pltpu.VMEM((3, kvh, 8, lanes), f32),
            pltpu.VMEM((2 * kvh, count * rows, group * head_size), bf16),
            pltpu.VMEM(w_out.shape, bf16),
            pltpu.VMEM((2, splits, share_rows, columns), f32),
            pltpu.VMEM((2, splits - 1, share_rows, columns), bf16),
            pltpu.VMEM((2 * splits - 2, share_rows, columns), bf16),
            dma((3 * kvh,)),
            dma((1,)),
            dma((3 * kvh,)),
            dma((3 * kvh,)),
            dma((4 * kvh,)),
            visits, visits, visits, visits, visits,
            sets,
            sets,
            dma((chunks * half * half,)),
            sets, sets,
            sets, sets,
            dma((2 * splits - 2,)),
            dma((2 * splits - 2,)),
        ],
        compiler_params=pltpu.CompilerParams(
            collective_id=0, has_side_effects=True, vmem_limit_bytes=60 << 20
        ),
    )(q, prefix_keys, cached_prefix_values, shard_len, reach, w_out)


def solution(mesh):
    return jax.shard_map(
        on_device,
        mesh=mesh,
        in_specs=(
            P("blk", "heads", None),
            P("heads", "blk", None),
            P("heads", "blk", None),
            P(),
            P(),
            P("heads", "blk"),
        ),
        out_specs=P("heads", "blk"),
        check_vma=False,
    )
```

```python
import functools
import math

import jax
import jax.numpy as jnp
from jax import lax
from jax.experimental import pallas as pl
from jax.experimental.pallas import tpu as pltpu
from jax.sharding import PartitionSpec as P

masked_score = -1e30

LOCAL = (((0, 0, 1, 0),), ((1, 1, 1, 1),))
OWN = (((0, 1, 0, 1), (1, 1, 1, 1)), ((0, 0, 1, 0), (0, 1, 0, 1)))
VISIT = ((2, 0, 1, 0), (2, 1, 0, 1), (3, 0, 1, 0), (3, 1, 0, 1), (4, 0, 1, 1))
SLOT_BLOCK = (0, 1, -2, -1, -3)


def pick(index, values):
    out = jnp.int32(values[-1])
    for n in range(len(values) - 2, -1, -1):
        out = jnp.where(index == n, jnp.int32(values[n]), out)
    return out


def layer_kernel(row_sets, rows, q_ref, k_ref, v_ref, live_ref, reach_ref, w_ref, o_ref,
                 q_all, k_all, v_all, run_max, run_sum, run_acc, own_part, own_stat,
                 part_out, stat_out, part_in, stat_in, buf, w_buf, acc, outgoing, incoming,
                 local_sem, w_sem, kv_send, kv_recv, q_send, q_recv, part_send, part_recv, stat_send, stat_recv,
                 col_send, col_recv, forward_send, pair_send, pair_recv, core_send, core_recv,
                 share_send, share_recv):
    splits = lax.axis_size("heads")
    count = lax.axis_size("blk")
    h = lax.axis_index("heads")
    me = lax.axis_index("blk")
    chips = count // 2
    chip, c = me // 2, me % 2
    r, p = chip // 2, chip % 2
    half = row_sets // 2
    _, kvh, lanes, head_size = q_ref.shape
    group = lanes // rows
    keys = k_ref.shape[1]
    kv_split = k_ref.shape[0] // kvh
    wide = group * head_size
    band = 4 * rows
    per_share = row_sets // splits
    share_rows = 2 * per_share * rows
    columns = w_ref.shape[1]
    strip = min(1024, columns)
    first = ((h + 1) % splits) * per_share
    chunks = 2 * kvh
    outgoing_sets = row_sets - per_share
    outgoing_half = (outgoing_sets + 1) // 2
    gateway = half - 1 + r // half
    other_gateway = half - r // half
    my_half = (r // half) * half

    def device(row_set, pair, core):
        return (row_set * 2 + pair) * 2 + core

    def remote(src, dst, sent, landed, head, blk):
        return pltpu.make_async_remote_copy(
            src_ref=src, dst_ref=dst, send_sem=sent, recv_sem=landed,
            device_id=(head, blk), device_id_type=pl.DeviceIdType.MESH,
        )

    def kv_half(core, i):
        return core * (kv_split - 1) * kvh + i

    def local(i):
        return [
            pltpu.make_async_copy(k_ref.at[kv_half(c, i)], k_all.at[c, i], local_sem.at[3 * i]),
            pltpu.make_async_copy(v_ref.at[kv_half(c, i)], v_all.at[c, i], local_sem.at[3 * i + 1]),
            pltpu.make_async_copy(q_ref.at[c, i], q_all.at[c, i], local_sem.at[3 * i + 2]),
        ]

    def swapped(i, shard):
        return [
            remote(k_ref.at[kv_half(1 - c, i)], k_all.at[shard, i], kv_send.at[3 * i], kv_recv.at[3 * i], h, me + 1 - 2 * c),
            remote(v_ref.at[kv_half(1 - c, i)], v_all.at[shard, i], kv_send.at[3 * i + 1], kv_recv.at[3 * i + 1], h, me + 1 - 2 * c),
            remote(q_ref.at[1 - c, i], q_all.at[shard, i], kv_send.at[3 * i + 2], kv_recv.at[3 * i + 2], h, me + 1 - 2 * c),
        ]

    def visit(i, core, slot, ahead):
        at = (i * 2 + core) * 2 + ahead - 1
        return remote(q_ref.at[core, i], q_all.at[slot, i], q_send.at[at], q_recv.at[(slot - 2) * kvh + i],
                      h, 2 * ((chip + ahead) % chips) + core)

    def part_home(v, i):
        back = 1 + v // 2
        return remote(part_out.at[v, i], part_in.at[v, i], part_send.at[v * kvh + i], part_recv.at[v * kvh + i],
                      h, 2 * ((chip - back + chips) % chips) + c)

    def stat_home(v, i):
        back = 1 + v // 2
        return remote(stat_out.at[v, i], stat_in.at[v, i], stat_send.at[v * kvh + i], stat_recv.at[v * kvh + i],
                      h, 2 * ((chip - back + chips) % chips) + c)

    def view(n, row_set, pair):
        at = (((n % 2) * row_sets + row_set) * 2 + pair) * rows
        return buf.at[c * kvh + n // 2, pl.ds(pl.multiple_of(at, rows), rows), :]

    def to_column(n, row_set, target, sent):
        spot = view(n, row_set, p)
        return remote(spot, spot, sent, col_recv.at[n * row_sets + row_set], h, device(target, p, c))

    def to_pair(n, row_set, pair):
        spot = view(n, row_set, pair)
        at = n * row_sets + row_set
        return remote(spot, spot, pair_send.at[at], pair_recv.at[at], h, device(r, 1 - p, c))

    def to_core(n, row_set, core):
        at = pl.multiple_of(((n % 2) * row_sets + row_set) * 2 * rows, 2 * rows)
        spot = buf.at[core * kvh + n // 2, pl.ds(at, 2 * rows), :]
        at = n * row_sets + row_set
        return remote(spot, spot, core_send.at[at], core_recv.at[at], h, device(r, p, 1 - c))

    def to_share(e, j):
        owner = (h + 1 + j) % splits
        slot = e * (splits - 1) + splits - 2 - j
        return remote(outgoing.at[e, j], incoming.at[slot], share_send.at[e * (splits - 1) + j], share_recv.at[slot],
                      owner, me)

    def from_share(slot):
        return remote(outgoing.at[0, 0], incoming.at[slot], share_send.at[0], share_recv.at[slot],
                      (h + 1) % splits, me)

    def unicast(n):
        return n < 0

    def own_columns(n, act):
        for d in range(1, row_sets):
            target = (r + d) % row_sets

            @pl.when((target // half == r // half) | (target == other_gateway) | unicast(n))
            def _():
                act(to_column(n, r, target, col_send.at[n * row_sets + d]))

    def forwards(n, row_set):
        base = (n * half + row_set % half) * half
        return [to_column(n, row_set, my_half + (r - my_half + d) % half, forward_send.at[base + d])
                for d in range(1, half)]

    for i in range(kvh):
        for copy in local(i):
            copy.start()
    greeted = [(h, device((r + d) % row_sets, p, c)) for d in range(1, row_sets)]
    greeted += [(h, device(r, 1 - p, c)), (h, me + 1 - 2 * c)]
    greeted += [((h + d) % splits, me) for d in range(1, splits)]
    for d in (1, 2, chips - 2, chips - 1):
        greeted += [(h, 2 * ((chip + d) % chips) + core) for core in range(2)]
    barrier = pltpu.get_barrier_semaphore()
    for peer in greeted:
        pl.semaphore_signal(barrier, inc=1, device_id=peer, device_id_type=pl.DeviceIdType.MESH)
    def start_visits(i):
        for core in range(2):
            visit(i, core, 2 + c, 1).start()

            @pl.when(c == 1)
            def _():
                visit(i, core, 4, 2).start()

    w_copy = pltpu.make_async_copy(w_ref, w_buf, w_sem.at[0])

    factor = head_size**-0.5 * math.log2(math.e)

    last = kvh - 1

    def attend(i, what):
        slot, shard, begins, ends = what
        held = jnp.where(slot < 2, i, kvh)
        ahead = pick(slot, SLOT_BLOCK)
        owner = (2 * chip + ahead + count) % count
        edge = reach_ref[owner] - (shard - ahead) * keys
        live = live_ref[2 * chip + shard]
        token = lax.broadcasted_iota(jnp.int32, (1, lanes), 1) % rows
        limit = jnp.minimum(edge + token, live)
        seen = lax.broadcasted_iota(jnp.int32, (keys, lanes), 0) < limit
        s = lax.dot_general(
            k_all[shard, i], q_all[slot, i], (((1,), (1,)), ((), ())), preferred_element_type=jnp.float32
        )
        s = jnp.where(seen, s * factor, masked_score)
        m = jnp.max(s, axis=0, keepdims=True)
        weight = jnp.exp2(s - m)
        total = jnp.sum(weight, axis=0, keepdims=True)
        part = lax.dot_general(
            v_all[shard, i], weight.astype(jnp.bfloat16), (((0,), (0,)), ((), ())),
            preferred_element_type=jnp.float32,
        )

        @pl.when(begins == 1)
        def _():
            run_max[held] = jnp.broadcast_to(m, run_max.shape[1:])
            run_sum[held] = jnp.broadcast_to(total, run_sum.shape[1:])
            run_acc[held] = part

        @pl.when(begins == 0)
        def _():
            before = run_max[held, :1, :]
            joined = jnp.maximum(before, m)
            old, new = jnp.exp2(before - joined), jnp.exp2(m - joined)
            run_max[held] = jnp.broadcast_to(joined, run_max.shape[1:])
            run_sum[held] = jnp.broadcast_to(run_sum[held, :1, :] * old + total * new, run_sum.shape[1:])
            run_acc[held] = run_acc[held] * old + part * new

        @pl.when((ends == 1) & (slot < 2))
        def _():
            own_part[slot, i] = run_acc[held] * (1.0 / run_sum[held, :1, :])
            own_stat[slot, i] = run_max[held] + jnp.log2(run_sum[held])

        @pl.when((ends == 1) & (slot >= 2))
        def _():
            part_out[slot - 2, i] = (run_acc[held] * (1.0 / run_sum[held, :1, :])).astype(part_out.dtype)
            stat_out[slot - 2, i] = run_max[held] + jnp.log2(run_sum[held])

    def merge(i, e):
        arrived = [e] if e == 0 else [1, 2]
        for v in arrived:
            part_home(v, i).wait_recv()
            stat_home(v, i).wait_recv()
        stats = [own_stat[e, i, :1, :]] + [stat_in[v, i, :1, :] for v in arrived]
        joined = functools.reduce(jnp.maximum, stats)
        weights = [jnp.exp2(s - joined) for s in stats]
        inverse = 1.0 / functools.reduce(jnp.add, weights)
        total = own_part[e, i] * (weights[0] * inverse)
        for v, weight in zip(arrived, weights[1:]):
            total = total + part_in[v, i].astype(jnp.float32) * (weight * inverse)
        total = total.T.astype(jnp.bfloat16)
        spot = pl.ds(pl.multiple_of(((e * row_sets + r) * 2 + p) * rows, rows), rows)
        for g in range(group):
            buf[c * kvh + i, spot, g * head_size : (g + 1) * head_size] = total[g * rows : (g + 1) * rows]
        n = 2 * i + e
        own_columns(n, lambda copy: copy.start())
        if not (i is last and e == 1):
            to_pair(n, r, p).start()

    def direct(n, row_set):
        return (row_set // half == r // half) | (r == gateway) | unicast(n)

    def relay_one(n, row_set):
        to_column(n, row_set, r, col_send.at[0]).wait_recv()
        to_pair(n, row_set, p).start()

        @pl.when((row_set // half != r // half) & (r == gateway) & jnp.logical_not(unicast(n)))
        def _():
            for copy in forwards(n, row_set):
                copy.start()

    def relay_some(n, start, stop, direct_now, own_too=False):
        def some(k, carry):
            row_set = (first + k) % row_sets

            @pl.when((direct(n, row_set) == direct_now) & (row_set != r))
            def _():
                relay_one(n, row_set)

            if direct_now and own_too:
                @pl.when(row_set == r)
                def _():
                    to_pair(n, r, p).start()

            return carry

        lax.fori_loop(start, stop, some, 0)

    def relay_all(n, start, stop, own_too=False):
        relay_some(n, start, stop, True, own_too)
        relay_some(n, start, stop, False)

    here, span = kvh, len(OWN[0]) + len(VISIT)
    steps = here + span * kvh

    def unit(s, carry):
        early = s < here
        i = jnp.where(early, s, (s - here) // span)
        j = jnp.where(early, 0, (s - here) % span)
        own = jnp.logical_not(early) & (j < len(OWN[0]))
        visiting = jnp.logical_not(early) & (j >= len(OWN[0]))
        j = jnp.where(visiting, j - len(OWN[0]), j)

        @pl.when(early)
        def _():
            for copy in local(i):
                copy.wait()

        @pl.when(s == here)
        def _():
            pl.semaphore_wait(barrier, len(greeted))
            for copy in swapped(0, c):
                copy.start()
            start_visits(0)

        for n in range(1, kvh):
            @pl.when(s == here + 1 + span * (n - 1))
            def _():
                for copy in swapped(n, c):
                    copy.start()

            @pl.when(s == here + 3 + span * (n - 1))
            def _():
                start_visits(n)

        @pl.when(s == here + 4)
        def _():
            w_copy.start()

        @pl.when(jnp.logical_not(early) & ((s - here) % span == 0))
        def _():
            for copy in swapped(i, 1 - c):
                copy.wait_recv()

        for at, slot in ((0, 2), (2, 3), (4, 4)):
            @pl.when(visiting & (j == at))
            def _():
                visit(i, 0, slot, 1).wait_recv()

        def choose(field):
            local_one = pick(c, [LOCAL[core][0][field] for core in range(2)])
            own_one = pick(2 * c + j, [OWN[core][n][field] for core in range(2) for n in range(2)])
            visit_one = pick(j, [what[field] for what in VISIT])
            return jnp.where(early, local_one, jnp.where(own, own_one, visit_one))

        attend(i, [choose(field) for field in range(4)])
        for at, v in ((1, 0), (3, 1), (4, 2)):
            @pl.when(visiting & (j == at))
            def _():
                part_home(v, i).start()
                stat_home(v, i).start()

        @pl.when(own & (j == 0) & (i > 0))
        def _():
            merge(i - 1, 0)

        @pl.when(visiting & (j == 1) & (i > 0))
        def _():
            merge(i - 1, 1)
            relay_some(2 * i - 2, 0, outgoing_sets, True)

        @pl.when(visiting & (j == 3) & (i > 0))
        def _():
            relay_some(2 * i - 2, 0, outgoing_sets, False)
            relay_some(2 * i - 2, outgoing_sets, row_sets, True)

        @pl.when(visiting & (j == 4) & (i == last))
        def _():
            merge(i, 0)

            @pl.when(i > 0)
            def _():
                relay_some(2 * i - 2, outgoing_sets, row_sets, False)
                relay_some(2 * i - 1, 0, row_sets, True)

        return carry

    lax.fori_loop(0, steps, unit, 0)
    late = chunks - 2
    def over(start, stop, act):
        def some(k, carry):
            act(k)
            return carry

        lax.fori_loop(start, stop, some, 0)

    def spread(n, start, stop):
        def some(k):
            row_set = (first + k) % row_sets
            to_pair(n, row_set, 1 - p).wait_recv()
            to_core(n, row_set, c).start()

        over(start, stop, some)

    def project(n, j):
        i, e = n // 2, n % 2
        owner = (h + 1 + j) % splits
        over(0, per_share, lambda x: to_core(n, owner * per_share + x, 1 - c).wait_recv())
        at = pl.multiple_of((e * row_sets + owner * per_share) * 2 * rows, 2 * rows)

        def multiply(n, carry):
            cols = pl.ds(pl.multiple_of(n * strip, strip), strip)
            value = sum(
                jnp.dot(
                    buf[core * kvh + i, pl.ds(at, share_rows), :],
                    w_buf[pl.ds(pl.multiple_of((core * kvh + i) * wide, wide), wide), cols],
                    preferred_element_type=jnp.float32,
                )
                for core in range(2)
            )

            @pl.when(i == 0)
            def _():
                acc[e, j, :, cols] = value

            @pl.when(i > 0)
            def _():
                acc[e, j, :, cols] += value

            return carry

        lax.fori_loop(0, columns // strip, multiply, 0)

    def send_share(e):
        def some(j):
            outgoing[e, j] = acc[e, j].astype(outgoing.dtype)
            to_share(e, j).start()

        over(0, splits - 1, some)

    def take_share(e):
        value = acc[e, splits - 1]
        for d in range(splits - 1):
            slot = e * (splits - 1) + d
            from_share(slot).wait_recv()
            value = value + incoming[slot].astype(jnp.float32)
        value = value.astype(o_ref.dtype)
        for x in range(per_share):
            for pair in range(2):
                at = x * band + (2 * pair + e) * rows
                o_ref[at : at + rows, :] = value[(2 * x + pair) * rows : (2 * x + pair + 1) * rows]

    def project_out(n):
        over(0, splits - 1, lambda j: project(n, j))

    if kvh > 1:
        relay_some(late - 1, 0, row_sets, False)
    merge(last, 1)
    relay_all(late, 0, outgoing_sets)
    w_copy.wait()
    for n in range(0, late, 2):
        spread(n, 0, outgoing_sets)
    relay_some(chunks - 1, 0, outgoing_sets, True, True)
    for n in range(0, late, 2):
        project_out(n)
    spread(late, 0, outgoing_sets)
    project_out(late)
    send_share(0)
    relay_some(chunks - 1, 0, outgoing_sets, False)
    for n in range(1, late, 2):
        spread(n, 0, outgoing_sets)
        project_out(n)
    spread(chunks - 1, 0, outgoing_sets)
    relay_all(late, outgoing_sets, row_sets)
    project_out(chunks - 1)
    send_share(1)
    relay_all(chunks - 1, outgoing_sets, row_sets, True)
    over(0, late, lambda n: spread(n, outgoing_sets, row_sets))
    over(0, late, lambda n: project(n, splits - 1))
    spread(late, outgoing_sets, row_sets)
    project(late, splits - 1)
    spread(chunks - 1, outgoing_sets, row_sets)
    take_share(0)
    project(chunks - 1, splits - 1)
    take_share(1)

    for i in range(kvh):
        for copy in swapped(i, c):
            copy.wait_send()
        for core in range(2):
            visit(i, core, 2 + c, 1).wait_send()

            @pl.when(c == 1)
            def _():
                visit(i, core, 4, 2).wait_send()

        for v in range(3):
            part_home(v, i).wait_send()
            stat_home(v, i).wait_send()

    def drain_sent(n, carry):
        own_columns(n, lambda copy: copy.wait_send())

        def some(row_set, carry):
            to_pair(n, row_set, p).wait_send()

            @pl.when((row_set // half != r // half) & (r == gateway) & jnp.logical_not(unicast(n)))
            def _():
                for copy in forwards(n, row_set):
                    copy.wait_send()

            return carry

        return lax.fori_loop(0, row_sets, some, carry)

    lax.fori_loop(0, chunks, drain_sent, 0)

    def drain_core(n, carry):
        to_core(n // row_sets, n % row_sets, c).wait_send()
        return carry

    lax.fori_loop(0, chunks * row_sets, drain_core, 0)

    for e in range(2):
        for j in range(splits - 1):
            to_share(e, j).wait_send()


def on_device(queries, prefix_keys, cached_prefix_values, shard_len, reach, w_out):
    count, splits = lax.axis_size("blk"), lax.axis_size("heads")
    rows, heads_local, head_size = queries.shape
    kv_local, keys_len = prefix_keys.shape[:2]
    kvh = kv_local // 2 if kv_local % 2 == 0 else kv_local
    group = heads_local // 2 // kvh
    lanes = group * rows
    columns = w_out.shape[1]
    row_sets = count // 4
    half = row_sets // 2
    per_share = row_sets // splits
    band = 4 * rows
    share_rows = 2 * per_share * rows
    chunks = 2 * kvh
    q = queries.reshape(rows, 2, kvh, group, head_size).transpose(1, 2, 3, 0, 4).reshape(2, kvh, lanes, head_size)
    dma = pltpu.SemaphoreType.DMA
    bf16, f32 = jnp.bfloat16, jnp.float32
    anywhere = pl.BlockSpec(memory_space=pl.ANY)
    scalars = pl.BlockSpec(memory_space=pltpu.SMEM)
    visits = dma((3 * kvh,))
    sets = dma((chunks * row_sets,))
    return pl.pallas_call(
        functools.partial(layer_kernel, row_sets, rows),
        out_shape=jax.ShapeDtypeStruct((per_share * band, columns), bf16),
        in_specs=[anywhere, anywhere, anywhere, scalars, scalars, anywhere],
        out_specs=pl.BlockSpec(memory_space=pltpu.VMEM),
        scratch_shapes=[
            pltpu.VMEM((5, kvh, lanes, head_size), bf16),
            pltpu.VMEM((2, kvh, keys_len, head_size), bf16),
            pltpu.VMEM((2, kvh, keys_len, head_size), bf16),
            pltpu.VMEM((kvh + 1, 8, lanes), f32),
            pltpu.VMEM((kvh + 1, 8, lanes), f32),
            pltpu.VMEM((kvh + 1, head_size, lanes), f32),
            pltpu.VMEM((2, kvh, head_size, lanes), f32),
            pltpu.VMEM((2, kvh, 8, lanes), f32),
            pltpu.VMEM((3, kvh, head_size, lanes), bf16),
            pltpu.VMEM((3, kvh, 8, lanes), f32),
            pltpu.VMEM((3, kvh, head_size, lanes), bf16),
            pltpu.VMEM((3, kvh, 8, lanes), f32),
            pltpu.VMEM((2 * kvh, count * rows, group * head_size), bf16),
            pltpu.VMEM(w_out.shape, bf16),
            pltpu.VMEM((2, splits, share_rows, columns), f32),
            pltpu.VMEM((2, splits - 1, share_rows, columns), bf16),
            pltpu.VMEM((2 * splits - 2, share_rows, columns), bf16),
            dma((3 * kvh,)),
            dma((1,)),
            dma((3 * kvh,)),
            dma((3 * kvh,)),
            dma((4 * kvh,)),
            visits, visits, visits, visits, visits,
            sets,
            sets,
            dma((chunks * half * half,)),
            sets, sets,
            sets, sets,
            dma((2 * splits - 2,)),
            dma((2 * splits - 2,)),
        ],
        compiler_params=pltpu.CompilerParams(
            collective_id=0, has_side_effects=True, vmem_limit_bytes=60 << 20
        ),
    )(q, prefix_keys, cached_prefix_values, shard_len, reach, w_out)


def solution(mesh):
    return jax.shard_map(
        on_device,
        mesh=mesh,
        in_specs=(
            P("blk", "heads", None),
            P("heads", "blk", None),
            P("heads", "blk", None),
            P(),
            P(),
            P("heads", "blk"),
        ),
        out_specs=P("heads", "blk"),
        check_vma=False,
    )
```

```python
import functools
import math

import jax
import jax.numpy as jnp
from jax import lax
from jax.experimental import pallas as pl
from jax.experimental.pallas import tpu as pltpu
from jax.sharding import PartitionSpec as P

masked_score = -1e30

LOCAL = (((0, 0, 1, 0),), ((1, 1, 1, 1),))
OWN = (((0, 1, 0, 1), (1, 1, 1, 1)), ((0, 0, 1, 0), (0, 1, 0, 1)))
VISIT = ((2, 0, 1, 0), (2, 1, 0, 1), (3, 0, 1, 0), (3, 1, 0, 1), (4, 0, 1, 1))
SLOT_BLOCK = (0, 1, -2, -1, -3)


def pick(index, values):
    out = jnp.int32(values[-1])
    for n in range(len(values) - 2, -1, -1):
        out = jnp.where(index == n, jnp.int32(values[n]), out)
    return out


def layer_kernel(row_sets, rows, q_ref, k_ref, v_ref, live_ref, reach_ref, w_ref, o_ref,
                 q_all, k_all, v_all, run_max, run_sum, run_acc, own_part, own_stat,
                 part_out, stat_out, part_in, stat_in, buf, w_buf, acc, outgoing, incoming,
                 local_sem, w_sem, kv_send, kv_recv, q_send, q_recv, part_send, part_recv, stat_send, stat_recv,
                 col_send, col_recv, forward_send, pair_send, pair_recv, core_send, core_recv,
                 share_send, share_recv):
    splits = lax.axis_size("heads")
    count = lax.axis_size("blk")
    h = lax.axis_index("heads")
    me = lax.axis_index("blk")
    chips = count // 2
    chip, c = me // 2, me % 2
    r, p = chip // 2, chip % 2
    half = row_sets // 2
    _, kvh, lanes, head_size = q_ref.shape
    group = lanes // rows
    keys = k_ref.shape[1]
    kv_split = k_ref.shape[0] // kvh
    wide = group * head_size
    band = 4 * rows
    per_share = row_sets // splits
    share_rows = 2 * per_share * rows
    columns = w_ref.shape[1]
    strip = min(1024, columns)
    first = ((h + 1) % splits) * per_share
    chunks = 2 * kvh
    outgoing_sets = row_sets - per_share
    outgoing_half = (outgoing_sets + 1) // 2
    gateway = half - 1 + r // half
    other_gateway = half - r // half
    my_half = (r // half) * half

    def device(row_set, pair, core):
        return (row_set * 2 + pair) * 2 + core

    def remote(src, dst, sent, landed, head, blk):
        return pltpu.make_async_remote_copy(
            src_ref=src, dst_ref=dst, send_sem=sent, recv_sem=landed,
            device_id=(head, blk), device_id_type=pl.DeviceIdType.MESH,
        )

    def kv_half(core, i):
        return core * (kv_split - 1) * kvh + i

    def local(i):
        return [
            pltpu.make_async_copy(k_ref.at[kv_half(c, i)], k_all.at[c, i], local_sem.at[3 * i]),
            pltpu.make_async_copy(v_ref.at[kv_half(c, i)], v_all.at[c, i], local_sem.at[3 * i + 1]),
            pltpu.make_async_copy(q_ref.at[c, i], q_all.at[c, i], local_sem.at[3 * i + 2]),
        ]

    def swapped(i, shard):
        return [
            remote(k_ref.at[kv_half(1 - c, i)], k_all.at[shard, i], kv_send.at[3 * i], kv_recv.at[3 * i], h, me + 1 - 2 * c),
            remote(v_ref.at[kv_half(1 - c, i)], v_all.at[shard, i], kv_send.at[3 * i + 1], kv_recv.at[3 * i + 1], h, me + 1 - 2 * c),
            remote(q_ref.at[1 - c, i], q_all.at[shard, i], kv_send.at[3 * i + 2], kv_recv.at[3 * i + 2], h, me + 1 - 2 * c),
        ]

    def visit(i, core, slot, ahead):
        at = (i * 2 + core) * 2 + ahead - 1
        return remote(q_ref.at[core, i], q_all.at[slot, i], q_send.at[at], q_recv.at[(slot - 2) * kvh + i],
                      h, 2 * ((chip + ahead) % chips) + core)

    def part_home(v, i):
        back = 1 + v // 2
        return remote(part_out.at[v, i], part_in.at[v, i], part_send.at[v * kvh + i], part_recv.at[v * kvh + i],
                      h, 2 * ((chip - back + chips) % chips) + c)

    def stat_home(v, i):
        back = 1 + v // 2
        return remote(stat_out.at[v, i], stat_in.at[v, i], stat_send.at[v * kvh + i], stat_recv.at[v * kvh + i],
                      h, 2 * ((chip - back + chips) % chips) + c)

    def view(n, row_set, pair):
        at = (((n % 2) * row_sets + row_set) * 2 + pair) * rows
        return buf.at[c * kvh + n // 2, pl.ds(pl.multiple_of(at, rows), rows), :]

    def to_column(n, row_set, target, sent):
        spot = view(n, row_set, p)
        return remote(spot, spot, sent, col_recv.at[n * row_sets + row_set], h, device(target, p, c))

    def to_pair(n, row_set, pair):
        spot = view(n, row_set, pair)
        at = n * row_sets + row_set
        return remote(spot, spot, pair_send.at[at], pair_recv.at[at], h, device(r, 1 - p, c))

    def to_core(n, row_set, core):
        at = pl.multiple_of(((n % 2) * row_sets + row_set) * 2 * rows, 2 * rows)
        spot = buf.at[core * kvh + n // 2, pl.ds(at, 2 * rows), :]
        at = n * row_sets + row_set
        return remote(spot, spot, core_send.at[at], core_recv.at[at], h, device(r, p, 1 - c))

    def to_share(e, j):
        owner = (h + 1 + j) % splits
        slot = e * (splits - 1) + splits - 2 - j
        return remote(outgoing.at[e, j], incoming.at[slot], share_send.at[e * (splits - 1) + j], share_recv.at[slot],
                      owner, me)

    def from_share(slot):
        return remote(outgoing.at[0, 0], incoming.at[slot], share_send.at[0], share_recv.at[slot],
                      (h + 1) % splits, me)

    def unicast(n):
        return n < 0

    def own_columns(n, act):
        for d in range(1, row_sets):
            target = (r + d) % row_sets

            @pl.when((target // half == r // half) | (target == other_gateway) | unicast(n))
            def _():
                act(to_column(n, r, target, col_send.at[n * row_sets + d]))

    def forwards(n, row_set):
        base = (n * half + row_set % half) * half
        return [to_column(n, row_set, my_half + (r - my_half + d) % half, forward_send.at[base + d])
                for d in range(1, half)]

    for i in range(kvh):
        for copy in local(i):
            copy.start()
    greeted = [(h, device((r + d) % row_sets, p, c)) for d in range(1, row_sets)]
    greeted += [(h, device(r, 1 - p, c)), (h, me + 1 - 2 * c)]
    greeted += [((h + d) % splits, me) for d in range(1, splits)]
    for d in (1, 2, chips - 2, chips - 1):
        greeted += [(h, 2 * ((chip + d) % chips) + core) for core in range(2)]
    barrier = pltpu.get_barrier_semaphore()
    for peer in greeted:
        pl.semaphore_signal(barrier, inc=1, device_id=peer, device_id_type=pl.DeviceIdType.MESH)
    def start_visits(i):
        for core in range(2):
            visit(i, core, 2 + c, 1).start()

            @pl.when(c == 1)
            def _():
                visit(i, core, 4, 2).start()

    w_copy = pltpu.make_async_copy(w_ref, w_buf, w_sem.at[0])

    factor = head_size**-0.5 * math.log2(math.e)

    last = kvh - 1

    def attend(i, what):
        slot, shard, begins, ends = what
        held = jnp.where(slot < 2, i, kvh)
        ahead = pick(slot, SLOT_BLOCK)
        owner = (2 * chip + ahead + count) % count
        edge = reach_ref[owner] - (shard - ahead) * keys
        live = live_ref[2 * chip + shard]
        token = lax.broadcasted_iota(jnp.int32, (1, lanes), 1) % rows
        limit = jnp.minimum(edge + token, live)
        seen = lax.broadcasted_iota(jnp.int32, (keys, lanes), 0) < limit
        s = lax.dot_general(
            k_all[shard, i], q_all[slot, i], (((1,), (1,)), ((), ())), preferred_element_type=jnp.float32
        )
        s = jnp.where(seen, s * factor, masked_score)
        m = jnp.max(s, axis=0, keepdims=True)
        weight = jnp.exp2(s - m)
        total = jnp.sum(weight, axis=0, keepdims=True)
        part = lax.dot_general(
            v_all[shard, i], weight.astype(jnp.bfloat16), (((0,), (0,)), ((), ())),
            preferred_element_type=jnp.float32,
        )

        @pl.when(begins == 1)
        def _():
            run_max[held] = jnp.broadcast_to(m, run_max.shape[1:])
            run_sum[held] = jnp.broadcast_to(total, run_sum.shape[1:])
            run_acc[held] = part

        @pl.when(begins == 0)
        def _():
            before = run_max[held, :1, :]
            joined = jnp.maximum(before, m)
            old, new = jnp.exp2(before - joined), jnp.exp2(m - joined)
            run_max[held] = jnp.broadcast_to(joined, run_max.shape[1:])
            run_sum[held] = jnp.broadcast_to(run_sum[held, :1, :] * old + total * new, run_sum.shape[1:])
            run_acc[held] = run_acc[held] * old + part * new

        @pl.when((ends == 1) & (slot < 2))
        def _():
            own_part[slot, i] = run_acc[held] * (1.0 / run_sum[held, :1, :])
            own_stat[slot, i] = run_max[held] + jnp.log2(run_sum[held])

        @pl.when((ends == 1) & (slot >= 2))
        def _():
            part_out[slot - 2, i] = (run_acc[held] * (1.0 / run_sum[held, :1, :])).astype(part_out.dtype)
            stat_out[slot - 2, i] = run_max[held] + jnp.log2(run_sum[held])

    def merge(i, e):
        arrived = [e] if e == 0 else [1, 2]
        for v in arrived:
            part_home(v, i).wait_recv()
            stat_home(v, i).wait_recv()
        stats = [own_stat[e, i, :1, :]] + [stat_in[v, i, :1, :] for v in arrived]
        joined = functools.reduce(jnp.maximum, stats)
        weights = [jnp.exp2(s - joined) for s in stats]
        inverse = 1.0 / functools.reduce(jnp.add, weights)
        total = own_part[e, i] * (weights[0] * inverse)
        for v, weight in zip(arrived, weights[1:]):
            total = total + part_in[v, i].astype(jnp.float32) * (weight * inverse)
        total = total.T.astype(jnp.bfloat16)
        spot = pl.ds(pl.multiple_of(((e * row_sets + r) * 2 + p) * rows, rows), rows)
        for g in range(group):
            buf[c * kvh + i, spot, g * head_size : (g + 1) * head_size] = total[g * rows : (g + 1) * rows]
        n = 2 * i + e
        own_columns(n, lambda copy: copy.start())
        if not (i is last and e == 1):
            to_pair(n, r, p).start()

    def direct(n, row_set):
        return (row_set // half == r // half) | (r == gateway) | unicast(n)

    def relay_one(n, row_set):
        to_column(n, row_set, r, col_send.at[0]).wait_recv()
        to_pair(n, row_set, p).start()

        @pl.when((row_set // half != r // half) & (r == gateway) & jnp.logical_not(unicast(n)))
        def _():
            for copy in forwards(n, row_set):
                copy.start()

    def relay_some(n, start, stop, direct_now, own_too=False):
        def some(k, carry):
            row_set = (first + k) % row_sets

            @pl.when((direct(n, row_set) == direct_now) & (row_set != r))
            def _():
                relay_one(n, row_set)

            if direct_now and own_too:
                @pl.when(row_set == r)
                def _():
                    to_pair(n, r, p).start()

            return carry

        lax.fori_loop(start, stop, some, 0)

    def relay_all(n, start, stop, own_too=False):
        relay_some(n, start, stop, True, own_too)
        relay_some(n, start, stop, False)

    here, span = kvh, len(OWN[0]) + len(VISIT)
    steps = here + span * kvh

    def unit(s, carry):
        early = s < here
        i = jnp.where(early, s, (s - here) // span)
        j = jnp.where(early, 0, (s - here) % span)
        own = jnp.logical_not(early) & (j < len(OWN[0]))
        visiting = jnp.logical_not(early) & (j >= len(OWN[0]))
        j = jnp.where(visiting, j - len(OWN[0]), j)

        @pl.when(early)
        def _():
            for copy in local(i):
                copy.wait()

        @pl.when(s == here)
        def _():
            pl.semaphore_wait(barrier, len(greeted))
            start_visits(0)
            for copy in swapped(0, c):
                copy.start()

        for n in range(1, kvh):
            @pl.when(s == here + 1 + span * (n - 1))
            def _():
                for copy in swapped(n, c):
                    copy.start()

            @pl.when(s == here + 3 + span * (n - 1))
            def _():
                start_visits(n)

        @pl.when(s == here + 4)
        def _():
            w_copy.start()

        @pl.when(jnp.logical_not(early) & ((s - here) % span == 0))
        def _():
            for copy in swapped(i, 1 - c):
                copy.wait_recv()

        for at, slot in ((0, 2), (2, 3), (4, 4)):
            @pl.when(visiting & (j == at))
            def _():
                visit(i, 0, slot, 1).wait_recv()

        def choose(field):
            local_one = pick(c, [LOCAL[core][0][field] for core in range(2)])
            own_one = pick(2 * c + j, [OWN[core][n][field] for core in range(2) for n in range(2)])
            visit_one = pick(j, [what[field] for what in VISIT])
            return jnp.where(early, local_one, jnp.where(own, own_one, visit_one))

        attend(i, [choose(field) for field in range(4)])
        for at, v in ((1, 0), (3, 1), (4, 2)):
            @pl.when(visiting & (j == at))
            def _():
                part_home(v, i).start()
                stat_home(v, i).start()

        @pl.when(own & (j == 0) & (i > 0))
        def _():
            merge(i - 1, 0)

        @pl.when(visiting & (j == 1) & (i > 0))
        def _():
            merge(i - 1, 1)
            relay_some(2 * i - 2, 0, outgoing_sets, True)

        @pl.when(visiting & (j == 3) & (i > 0))
        def _():
            relay_some(2 * i - 2, 0, outgoing_sets, False)
            relay_some(2 * i - 2, outgoing_sets, row_sets, True)

        @pl.when(visiting & (j == 4) & (i == last))
        def _():
            merge(i, 0)

            @pl.when(i > 0)
            def _():
                relay_some(2 * i - 2, outgoing_sets, row_sets, False)
                relay_some(2 * i - 1, 0, row_sets, True)

        return carry

    lax.fori_loop(0, steps, unit, 0)
    late = chunks - 2
    def over(start, stop, act):
        def some(k, carry):
            act(k)
            return carry

        lax.fori_loop(start, stop, some, 0)

    def spread(n, start, stop):
        def some(k):
            row_set = (first + k) % row_sets
            to_pair(n, row_set, 1 - p).wait_recv()
            to_core(n, row_set, c).start()

        over(start, stop, some)

    def project(n, j):
        i, e = n // 2, n % 2
        owner = (h + 1 + j) % splits
        over(0, per_share, lambda x: to_core(n, owner * per_share + x, 1 - c).wait_recv())
        at = pl.multiple_of((e * row_sets + owner * per_share) * 2 * rows, 2 * rows)

        def multiply(n, carry):
            cols = pl.ds(pl.multiple_of(n * strip, strip), strip)
            value = sum(
                jnp.dot(
                    buf[core * kvh + i, pl.ds(at, share_rows), :],
                    w_buf[pl.ds(pl.multiple_of((core * kvh + i) * wide, wide), wide), cols],
                    preferred_element_type=jnp.float32,
                )
                for core in range(2)
            )

            @pl.when(i == 0)
            def _():
                acc[e, j, :, cols] = value

            @pl.when(i > 0)
            def _():
                acc[e, j, :, cols] += value

            return carry

        lax.fori_loop(0, columns // strip, multiply, 0)

    def send_share(e):
        def some(j):
            outgoing[e, j] = acc[e, j].astype(outgoing.dtype)
            to_share(e, j).start()

        over(0, splits - 1, some)

    def take_share(e):
        value = acc[e, splits - 1]
        for d in range(splits - 1):
            slot = e * (splits - 1) + d
            from_share(slot).wait_recv()
            value = value + incoming[slot].astype(jnp.float32)
        value = value.astype(o_ref.dtype)
        for x in range(per_share):
            for pair in range(2):
                at = x * band + (2 * pair + e) * rows
                o_ref[at : at + rows, :] = value[(2 * x + pair) * rows : (2 * x + pair + 1) * rows]

    def project_out(n):
        over(0, splits - 1, lambda j: project(n, j))

    if kvh > 1:
        relay_some(late - 1, 0, row_sets, False)
    merge(last, 1)
    relay_all(late, 0, outgoing_sets)
    w_copy.wait()
    for n in range(0, late, 2):
        spread(n, 0, outgoing_sets)
    relay_some(chunks - 1, 0, outgoing_sets, True, True)
    for n in range(0, late, 2):
        project_out(n)
    spread(late, 0, outgoing_sets)
    project_out(late)
    send_share(0)
    relay_some(chunks - 1, 0, outgoing_sets, False)
    for n in range(1, late, 2):
        spread(n, 0, outgoing_sets)
        project_out(n)
    spread(chunks - 1, 0, outgoing_sets)
    relay_all(late, outgoing_sets, row_sets)
    project_out(chunks - 1)
    send_share(1)
    relay_all(chunks - 1, outgoing_sets, row_sets, True)
    over(0, late, lambda n: spread(n, outgoing_sets, row_sets))
    over(0, late, lambda n: project(n, splits - 1))
    spread(late, outgoing_sets, row_sets)
    project(late, splits - 1)
    spread(chunks - 1, outgoing_sets, row_sets)
    take_share(0)
    project(chunks - 1, splits - 1)
    take_share(1)

    for i in range(kvh):
        for copy in swapped(i, c):
            copy.wait_send()
        for core in range(2):
            visit(i, core, 2 + c, 1).wait_send()

            @pl.when(c == 1)
            def _():
                visit(i, core, 4, 2).wait_send()

        for v in range(3):
            part_home(v, i).wait_send()
            stat_home(v, i).wait_send()

    def drain_sent(n, carry):
        own_columns(n, lambda copy: copy.wait_send())

        def some(row_set, carry):
            to_pair(n, row_set, p).wait_send()

            @pl.when((row_set // half != r // half) & (r == gateway) & jnp.logical_not(unicast(n)))
            def _():
                for copy in forwards(n, row_set):
                    copy.wait_send()

            return carry

        return lax.fori_loop(0, row_sets, some, carry)

    lax.fori_loop(0, chunks, drain_sent, 0)

    def drain_core(n, carry):
        to_core(n // row_sets, n % row_sets, c).wait_send()
        return carry

    lax.fori_loop(0, chunks * row_sets, drain_core, 0)

    for e in range(2):
        for j in range(splits - 1):
            to_share(e, j).wait_send()


def on_device(queries, prefix_keys, cached_prefix_values, shard_len, reach, w_out):
    count, splits = lax.axis_size("blk"), lax.axis_size("heads")
    rows, heads_local, head_size = queries.shape
    kv_local, keys_len = prefix_keys.shape[:2]
    kvh = kv_local // 2 if kv_local % 2 == 0 else kv_local
    group = heads_local // 2 // kvh
    lanes = group * rows
    columns = w_out.shape[1]
    row_sets = count // 4
    half = row_sets // 2
    per_share = row_sets // splits
    band = 4 * rows
    share_rows = 2 * per_share * rows
    chunks = 2 * kvh
    q = queries.reshape(rows, 2, kvh, group, head_size).transpose(1, 2, 3, 0, 4).reshape(2, kvh, lanes, head_size)
    dma = pltpu.SemaphoreType.DMA
    bf16, f32 = jnp.bfloat16, jnp.float32
    anywhere = pl.BlockSpec(memory_space=pl.ANY)
    scalars = pl.BlockSpec(memory_space=pltpu.SMEM)
    visits = dma((3 * kvh,))
    sets = dma((chunks * row_sets,))
    return pl.pallas_call(
        functools.partial(layer_kernel, row_sets, rows),
        out_shape=jax.ShapeDtypeStruct((per_share * band, columns), bf16),
        in_specs=[anywhere, anywhere, anywhere, scalars, scalars, anywhere],
        out_specs=pl.BlockSpec(memory_space=pltpu.VMEM),
        scratch_shapes=[
            pltpu.VMEM((5, kvh, lanes, head_size), bf16),
            pltpu.VMEM((2, kvh, keys_len, head_size), bf16),
            pltpu.VMEM((2, kvh, keys_len, head_size), bf16),
            pltpu.VMEM((kvh + 1, 8, lanes), f32),
            pltpu.VMEM((kvh + 1, 8, lanes), f32),
            pltpu.VMEM((kvh + 1, head_size, lanes), f32),
            pltpu.VMEM((2, kvh, head_size, lanes), f32),
            pltpu.VMEM((2, kvh, 8, lanes), f32),
            pltpu.VMEM((3, kvh, head_size, lanes), bf16),
            pltpu.VMEM((3, kvh, 8, lanes), f32),
            pltpu.VMEM((3, kvh, head_size, lanes), bf16),
            pltpu.VMEM((3, kvh, 8, lanes), f32),
            pltpu.VMEM((2 * kvh, count * rows, group * head_size), bf16),
            pltpu.VMEM(w_out.shape, bf16),
            pltpu.VMEM((2, splits, share_rows, columns), f32),
            pltpu.VMEM((2, splits - 1, share_rows, columns), bf16),
            pltpu.VMEM((2 * splits - 2, share_rows, columns), bf16),
            dma((3 * kvh,)),
            dma((1,)),
            dma((3 * kvh,)),
            dma((3 * kvh,)),
            dma((4 * kvh,)),
            visits, visits, visits, visits, visits,
            sets,
            sets,
            dma((chunks * half * half,)),
            sets, sets,
            sets, sets,
            dma((2 * splits - 2,)),
            dma((2 * splits - 2,)),
        ],
        compiler_params=pltpu.CompilerParams(
            collective_id=0, has_side_effects=True, vmem_limit_bytes=60 << 20
        ),
    )(q, prefix_keys, cached_prefix_values, shard_len, reach, w_out)


def solution(mesh):
    return jax.shard_map(
        on_device,
        mesh=mesh,
        in_specs=(
            P("blk", "heads", None),
            P("heads", "blk", None),
            P("heads", "blk", None),
            P(),
            P(),
            P("heads", "blk"),
        ),
        out_specs=P("heads", "blk"),
        check_vma=False,
    )
```
